32 devices in a mesh: layer: 4 (over y, core), lat: 8 (over z, x).
Axes of the slice: x: 2, y: 2, z: 4, core: 2. Of those that a mesh axis runs over, the one named last changes fastest.
Arguments:
- residuals: bfloat16 [4, 256, 2048], P(None, ('layer', 'lat')), may hold values from -1100 to 1100
- topk_slots: int32 [4, 256, 64], P(None, ('layer', 'lat')), may hold values from -1 to 32767, as said below
- dictionary: bfloat16 [4, 32768, 2048], P('layer', 'lat'), may hold values from -80 to 80
- enc_bias: float32 [4, 32768], P('layer', 'lat'), may hold values from 0.5 to 3
- dec_bias: float32 [4, 2048], P('layer'), may hold values from -5 to 5
- dead_ids: int32 [4, 128], P('layer'), may hold values from 0 to 32767, as said below
- seed_tokens: int32 [4, 128], P('layer'), may hold values from 0 to 255
Outputs:
- reconstruction: bfloat16 [4, 256, 2048], P(None, ('layer', 'lat'))
- unexplained: float32 [4], P('layer')
- latent_mass: float32 [4, 32768], P('layer', 'lat')
- new_rows: bfloat16 [4, 128, 2048], P('layer', 'lat')
- new_bias: float32 [4, 32768], P('layer', 'lat')
The draws below stay inside these ranges and needn't reach their ends.
Inputs may be any that keep to these rules, and one draw needn't show every extreme that they name: `topk_slots`: slot s of a token belongs to latent shard s // 8: it holds -1 or an id from (s // 8) * 4096 to (s // 8 + 1) * 4096 - 1. Every token has exactly 32 slots that are not -1; ids may repeat. In every layer some token fills all 8 slots of one shard. `dead_ids`: the 128 ids of one layer are distinct.
All inputs are finite; a program needn't handle non-finite values.
Results may differ from the reference program's by a relative error of at most 0.009.
Values may be sent and summed in bfloat16 or wider, within the bound.
No kernel may reach another device: no remote copies, remote signals or barrier semaphores. Data moves between devices by JAX's collectives and lax.ppermute only.
A program may use at most 128 MiB of HBM per device.

```python
import math
import jax
import jax.numpy as jnp
from jax import lax

D = 2048
LAT_DEV = 4096
LATENTS = 32768
K = 32
SLOTS = 64
TOK_DEV = 8
LAYERS = 4
TOKENS = 256
R = 128
N_LAT = 8


def draw_residuals(key, part):
    first, second, third = jax.random.split(key, 3)
    tok_index = jnp.arange(TOKENS)
    ramp = jnp.sqrt(1.0 + 2.0 * (tok_index // TOK_DEV % N_LAT).astype(jnp.float32) / max(N_LAT - 1, 1))
    rough = jnp.exp(jax.random.uniform(first, (LAYERS, TOKENS, 1), jnp.float32, 0.0, math.log(10.0)))
    column = jnp.exp(jax.random.uniform(second, (LAYERS, 1, D), jnp.float32, 0.0, math.log(10.0)))
    base = jnp.clip(jax.random.normal(third, (LAYERS, TOKENS, D), jnp.float32), -4.0, 4.0)
    return (base * rough * column * ramp[None, :, None]).astype(jnp.bfloat16)


def draw_topk_slots(key, part):
    first, second, third, fourth = jax.random.split(key, 4)
    row_count = LAYERS * TOKENS
    slot_cap = SLOTS // N_LAT
    row_keys = jax.random.split(first, row_count)
    ranks = jax.vmap(lambda subkey: jax.random.permutation(subkey, SLOTS))(row_keys).astype(jnp.int32)
    special_tok = jax.random.randint(second, (LAYERS,), 0, TOKENS)
    special_shard = jax.random.randint(third, (LAYERS,), 0, N_LAT)
    row_layer = jnp.arange(row_count) // TOKENS
    row_tok = jnp.arange(row_count) % TOKENS
    slot_shard = jnp.arange(SLOTS) // slot_cap
    boosted = (row_tok == special_tok[row_layer])[:, None] & (slot_shard[None, :] == special_shard[row_layer][:, None])
    score = ranks - SLOTS * boosted.astype(jnp.int32)
    order = jnp.argsort(jnp.argsort(score, axis=1, stable=True), axis=1, stable=True)
    is_live = order < K
    offsets = jax.random.randint(fourth, (row_count, SLOTS), 0, LAT_DEV)
    latent_ids = jnp.where(is_live, slot_shard[None, :] * LAT_DEV + offsets, -1)
    return latent_ids.reshape(LAYERS, TOKENS, SLOTS).astype(jnp.int32)


def draw_dictionary(key, part):
    first, second = jax.random.split(key, 2)
    lat_index = jnp.arange(LATENTS)
    ramp = jnp.sqrt(1.0 + 2.0 * (lat_index // LAT_DEV).astype(jnp.float32) / max(N_LAT - 1, 1))
    rough = jnp.exp(jax.random.uniform(first, (LAYERS, LATENTS, 1), jnp.float32, 0.0, math.log(10.0)))
    base = jnp.clip(jax.random.normal(second, (LAYERS, LATENTS, D), jnp.float32), -4.0, 4.0)
    return (base * rough * ramp[None, :, None]).astype(jnp.bfloat16)


def draw_dead_ids(key, part):
    layer_keys = jax.random.split(key, LAYERS)
    chosen = jax.vmap(lambda subkey: jax.random.permutation(subkey, LATENTS)[:R])(layer_keys)
    return chosen.astype(jnp.int32)


def with_ends(values, rng, least, high):
    longest = values.shape.index(max(values.shape))
    spots = []
    for shift in (0, 1):
        where = [jax.random.randint(jax.random.fold_in(rng, axis), (), 0, length) for axis, length in enumerate(values.shape)]
        where[longest] = (where[longest] + shift) % values.shape[longest]
        spots.append(tuple(where))
    return values.at[spots[0]].set(least).at[spots[1]].set(high)


def steps_of(rng, extent, cuts, low, largest):
    loudness = 1.0
    for dim, shards_of in cuts:
        heights = jax.random.uniform(jax.random.fold_in(jax.random.fold_in(rng, 6), dim), (shards_of,), jnp.float32, low / len(cuts), largest / len(cuts))
        loudness = loudness * jnp.repeat(jnp.exp(heights), extent[dim] // shards_of).reshape((-1,) + (1,) * (len(extent) - 1 - dim))
    return loudness


def centred(key, shape, width, reach, pieces=(), held_as=jnp.bfloat16):
    result = width * jax.random.normal(key, shape, jnp.float32)
    if pieces:
        result = result * steps_of(key, shape, pieces, -0.22, 0.18)
    return jnp.clip(result, -reach, reach).astype(held_as)


def setup_inputs(seed: int = 0) -> dict:
    splits = jax.random.split(jax.random.key(seed), 8)
    residuals = draw_residuals(jax.random.fold_in(splits[7], 71), 0)
    topk_slots = draw_topk_slots(jax.random.fold_in(splits[7], 71), 0)
    dictionary = draw_dictionary(jax.random.fold_in(splits[7], 71), 0)
    enc_bias = jnp.clip(0.5 + 2.5 * jax.random.uniform(splits[3], (LAYERS, LATENTS), jnp.float32) ** steps_of(splits[3], (LAYERS, LATENTS), ((0, 4), (1, 8)), -0.2, 0.2), 0.5, 3.0)
    dec_bias = centred(splits[4], (LAYERS, D), 1.0, 5.0, ((0, 4),), jnp.float32)
    dead_ids = draw_dead_ids(jax.random.fold_in(splits[7], 71), 0)
    seed_tokens = with_ends(jax.random.randint(splits[6], (LAYERS, R), 0, TOKENS), jax.random.fold_in(splits[6], 1), 0, TOKENS - 1).astype(jnp.int32)
    return dict(residuals=residuals, topk_slots=topk_slots, dictionary=dictionary, enc_bias=enc_bias, dec_bias=dec_bias, dead_ids=dead_ids, seed_tokens=seed_tokens)


def layer_terms(packed):
    normed, latent_ids, table, enc_row, dec_row, dead_row, seed_row = packed
    row_norms = jnp.sqrt(lax.optimization_barrier(jnp.sum(jnp.square(table.astype(jnp.float32)), axis=1)) + 1e-06)
    shifts = jnp.dot(table.astype(jnp.float32), dec_row, precision=lax.Precision.HIGHEST)
    is_live = latent_ids >= 0
    clipped = jnp.where(is_live, latent_ids, 0).astype(jnp.int32)

    def block_terms(block):
        feats, picks, live_block = block
        picked = jnp.take(table, picks, axis=0).astype(jnp.float32)
        products = jnp.einsum('td,tsd->ts', feats.astype(jnp.float32), picked, precision=lax.Precision.HIGHEST)
        preact = (products - shifts[picks]) / row_norms[picks] + enc_row[picks]
        activity = jnp.where(live_block, jnp.maximum(preact, 0.0), 0.0)
        rounded = lax.optimization_barrier((activity / row_norms[picks]).astype(jnp.bfloat16))
        coefficient = rounded.astype(jnp.float32)
        estimate = dec_row + jnp.einsum('ts,tsd->td', coefficient, picked, precision=lax.Precision.HIGHEST)
        return (estimate, activity)
    block_count = TOKENS // TOK_DEV
    estimate, activity = lax.map(block_terms, (normed.reshape(block_count, TOK_DEV, D), clipped.reshape(block_count, TOK_DEV, SLOTS), is_live.reshape(block_count, TOK_DEV, SLOTS)))
    estimate = estimate.reshape(TOKENS, D)
    activity = activity.reshape(TOKENS, SLOTS)
    feat32 = normed.astype(jnp.float32)
    errors = feat32 - estimate
    centered = feat32 - lax.optimization_barrier(jnp.mean(feat32, axis=0))
    unexplained = jnp.sum(jnp.square(errors)) / jnp.sum(jnp.square(centered))
    latent_mass = jax.ops.segment_sum(activity.reshape(-1), clipped.reshape(-1), num_segments=LATENTS)
    seeds = jnp.take(errors, seed_row, axis=0)
    seed_norm = jnp.sqrt(lax.optimization_barrier(jnp.sum(jnp.square(seeds), axis=1, keepdims=True)) + 1e-06)
    new_rows = (seeds / seed_norm * jnp.mean(row_norms)).astype(jnp.bfloat16)
    new_bias = enc_row.at[dead_row].set(0.0)
    return (estimate.astype(jnp.bfloat16), unexplained, latent_mass, new_rows, new_bias)

def reference(residuals, topk_slots, dictionary, enc_bias, dec_bias, dead_ids, seed_tokens):
    wide = residuals.astype(jnp.float32)
    mean_square = lax.optimization_barrier(jnp.mean(jnp.square(wide), axis=(1, 2)))
    normed = (wide * lax.rsqrt(mean_square)[:, None, None]).astype(jnp.bfloat16)
    reconstruction, unexplained, latent_mass, new_rows, new_bias = lax.map(layer_terms, (normed, topk_slots, dictionary, enc_bias, dec_bias, dead_ids, seed_tokens))
    return (reconstruction, unexplained, latent_mass, new_rows, new_bias)
```

```python
import functools
import jax
import jax.numpy as jnp
from jax import lax
from jax.experimental import pallas as pl
from jax.experimental.pallas import tpu as pltpu
from jax.sharding import PartitionSpec as P

F32 = jnp.float32
BF16 = jnp.bfloat16
LOW = 64
VMEM_SPEC = pl.BlockSpec(memory_space=pltpu.VMEM)
SMEM_SPEC = pl.BlockSpec(memory_space=pltpu.SMEM)


def split_lat(count):
    inner = 1
    while inner * inner * 4 <= count and count % (inner * 2) == 0:
        inner *= 2
    return count // inner, inner


def shift_to(value, axis, size, mask):
    return lax.ppermute(value, axis, [(i, i ^ mask) for i in range(size)])


def pack_kernel(groups, per_shard, lat_dev, group_ref, res_ref, slots_ref, *outs):
    group = group_ref[0]
    width = res_ref.shape[2]
    slot_count = slots_ref.shape[2]
    shard = lax.broadcasted_iota(jnp.int32, slots_ref.shape[1:], 1) // per_shard
    for mask in range(groups):
        layer = jnp.bitwise_xor(group, mask)
        slots = slots_ref[layer]
        live = slots >= 0
        local = slots - shard * lat_dev
        high = jnp.where(live, local // LOW, -1)
        low = jnp.where(live, local % LOW, 0)
        outs[mask][:, :width] = res_ref[layer]
        outs[mask][:, width : width + 2 * slot_count] = jnp.concatenate([high, low], axis=1).astype(F32).astype(BF16)


def pack(group, residuals, slots, per_shard, lat_dev):
    groups, rows, width = residuals.shape
    out = jax.ShapeDtypeStruct((rows, width + 2 * slots.shape[2]), BF16)
    return pl.pallas_call(
        functools.partial(pack_kernel, groups, per_shard, lat_dev),
        out_shape=[out] * groups,
        in_specs=[SMEM_SPEC, VMEM_SPEC, VMEM_SPEC],
        out_specs=[VMEM_SPEC] * groups,
        name="pack",
    )(group, residuals, slots)


def norms_kernel(dict_ref, enc_ref, dec_ref, cols_ref, total_ref):
    rows = dict_ref.shape[0]
    tile = dict_ref[...].astype(F32)
    squares = jnp.sum(tile * tile, axis=1, keepdims=True)
    shift = jnp.sum(tile * dec_ref[...], axis=1, keepdims=True)
    norm = jnp.sqrt(squares + 1e-06)
    inverse = 1.0 / norm
    eye = lax.broadcasted_iota(jnp.int32, (128, 128), 0) == lax.broadcasted_iota(jnp.int32, (128, 128), 1)
    enc = jnp.concatenate(
        [
            jnp.sum(jnp.where(eye, enc_ref[:, k * 128 : (k + 1) * 128], 0.0), axis=1, keepdims=True)
            for k in range(rows // 128)
        ],
        axis=0,
    )
    offset = enc - shift * inverse
    lane = lax.broadcasted_iota(jnp.int32, (rows, 128), 1)
    cols_ref[...] = jnp.where(lane == 0, inverse, offset)

    @pl.when(pl.program_id(0) == 0)
    def _():
        total_ref[...] = jnp.zeros_like(total_ref)

    total_ref[...] += jnp.sum(norm)


def norms(dictionary, enc_bias, dec_bias, tile):
    lat_dev, width = dictionary.shape
    return pl.pallas_call(
        norms_kernel,
        grid=(lat_dev // tile,),
        out_shape=[
            jax.ShapeDtypeStruct((lat_dev, 128), F32),
            jax.ShapeDtypeStruct((8, 128), F32),
        ],
        in_specs=[
            pl.BlockSpec((tile, width), lambda i: (i, 0)),
            pl.BlockSpec((1, tile), lambda i: (0, i)),
            pl.BlockSpec((1, width), lambda i: (0, 0)),
        ],
        out_specs=[
            pl.BlockSpec((tile, 128), lambda i: (i, 0)),
            pl.BlockSpec((8, 128), lambda i: (0, 0)),
        ],
        name="norms",
    )(dictionary, enc_bias, dec_bias)


def main_kernel(blocks, per_shard, slot_count, r_dev, shard_ref, seed_ref, dict_ref, cols_ref, *refs):
    ins = refs[:blocks]
    shares = refs[blocks : 2 * blocks]
    normed_out, own_ref, mass_ref = refs[2 * blocks : 2 * blocks + 3]
    normed, ids, weights, estimate = refs[2 * blocks + 3 :]
    step = pl.program_id(0)
    tile, width = dict_ref.shape
    rows = ins[0].shape[0]
    tokens = rows * blocks

    @pl.when(step == 0)
    def _():
        total = jnp.zeros((1, 1), F32)
        for block in ins:
            raw = block[:, :width].astype(F32)
            total += jnp.sum(raw * raw, keepdims=True)
        scale = lax.rsqrt(total / (tokens * width))
        for k, block in enumerate(ins):
            normed[k * rows : (k + 1) * rows, :] = (block[:, :width].astype(F32) * scale).astype(BF16)
        coded = jnp.concatenate([block[:, width:] for block in ins], axis=0)
        slot = lax.broadcasted_iota(jnp.int32, (per_shard, 2 * slot_count), 0) + shard_ref[0] * per_shard
        column = lax.broadcasted_iota(jnp.int32, (per_shard, 2 * slot_count), 1)
        pick = lambda shift: lax.dot_general(
            jnp.where(column == slot + shift, 1.0, 0.0).astype(BF16),
            coded,
            (((1,), (1,)), ((), ())),
            preferred_element_type=F32,
        )
        ids_now = pick(0) * LOW + pick(slot_count)
        ids[...] = ids_now
        weights[...] = sum(jnp.where(ids_now == ids_now[c : c + 1], 1.0, 0.0) for c in range(per_shard))
        estimate[...] = jnp.zeros_like(estimate)

    products = lax.dot_general(
        dict_ref[...], normed[...], (((1,), (1,)), ((), ())), preferred_element_type=F32
    )
    latent = (lax.broadcasted_iota(jnp.int32, (tile, tokens), 0) + step * tile).astype(F32)
    count = jnp.zeros((tile, tokens), F32)
    for c in range(per_shard):
        count = jnp.where(latent == ids[c : c + 1, :], weights[c : c + 1, :], count)
    inverse = cols_ref[:, 0:1]
    activity = jnp.maximum(products * inverse + cols_ref[:, 1:2], 0.0)
    eye = lax.broadcasted_iota(jnp.int32, (128, 128), 0) == lax.broadcasted_iota(jnp.int32, (128, 128), 1)
    mass = jnp.sum(activity * count, axis=1, keepdims=True)
    for k in range(tile // 128):
        mass_ref[:, k * 128 : (k + 1) * 128] = jnp.sum(
            jnp.where(eye, mass[k * 128 : (k + 1) * 128], 0.0), axis=0, keepdims=True
        )
    coefficient = (activity * inverse).astype(BF16) * count.astype(BF16)
    estimate[...] += lax.dot_general(
        coefficient, dict_ref[...], (((0,), (0,)), ((), ())), preferred_element_type=F32
    )

    @pl.when(step == pl.num_programs(0) - 1)
    def _():
        share = estimate[...].astype(BF16)
        place = lax.broadcasted_iota(jnp.int32, (tokens, r_dev * blocks), 0)
        chosen = jnp.where(place == seed_ref[...], 1.0, 0.0).astype(BF16)
        seeds = lax.dot_general(chosen, share, (((0,), (0,)), ((), ())), preferred_element_type=F32).astype(BF16)
        seed_features = lax.dot_general(
            chosen, normed[...], (((0,), (0,)), ((), ())), preferred_element_type=F32
        ).astype(BF16)
        for k in range(blocks):
            shares[k][:rows] = share[k * rows : (k + 1) * rows]
            shares[k][rows:] = seeds[k * r_dev : (k + 1) * r_dev]
        own_ref[:rows] = normed[:rows]
        own_ref[rows:] = seed_features[:r_dev]
        normed_out[...] = normed[...]


def main(shard, seed_places, dictionary, cols, blocks, per_shard, slot_count, tile):
    lat_dev, width = dictionary.shape
    count = len(blocks)
    rows = blocks[0].shape[0]
    tokens = rows * count
    r_dev = seed_places.shape[1] // count
    share = jax.ShapeDtypeStruct((rows + r_dev, width), BF16)
    whole = lambda shape: pl.BlockSpec(shape, lambda i: (0,) * len(shape))
    return pl.pallas_call(
        functools.partial(main_kernel, count, per_shard, slot_count, r_dev),
        grid=(lat_dev // tile,),
        out_shape=[share] * count
        + [
            jax.ShapeDtypeStruct((tokens, width), BF16),
            share,
            jax.ShapeDtypeStruct((1, lat_dev), F32),
        ],
        in_specs=[
            SMEM_SPEC,
            whole(seed_places.shape),
            pl.BlockSpec((tile, width), lambda i: (i, 0)),
            pl.BlockSpec((tile, 128), lambda i: (i, 0)),
        ]
        + [whole(blocks[0].shape)] * count,
        out_specs=[whole(share.shape)] * count
        + [
            whole((tokens, width)),
            whole(share.shape),
            pl.BlockSpec((1, tile), lambda i: (0, i)),
        ],
        scratch_shapes=[
            pltpu.VMEM((tokens, width), BF16),
            pltpu.VMEM((per_shard, tokens), F32),
            pltpu.VMEM((per_shard, tokens), F32),
            pltpu.VMEM((tokens, width), F32),
        ],
        name="sparse_code",
    )(shard, seed_places, dictionary, cols, *blocks)


def finish_kernel(parts, groups, latents, own_ref, dec_ref, norm_ref, *refs):
    shares = refs[:parts]
    recon = refs[parts : parts + groups]
    rows_ref, numerator_ref = refs[parts + groups :]
    r_dev = rows_ref.shape[0]
    rows = own_ref.shape[0] - r_dev
    summed = shares[0][...].astype(F32)
    for share in shares[1:]:
        summed += share[...].astype(F32)
    estimate = summed + dec_ref[...]
    errors = own_ref[...].astype(F32) - estimate
    size = rows // groups
    for k in range(groups):
        recon[k][...] = estimate[k * size : (k + 1) * size].astype(BF16)
    own = errors[:rows]
    numerator_ref[...] = jnp.full(numerator_ref.shape, jnp.sum(own * own), F32)
    seeds = errors[rows:]
    norm = jnp.sqrt(jnp.sum(seeds * seeds, axis=1, keepdims=True) + 1e-06)
    rows_ref[...] = (seeds / norm * (norm_ref[0:1, 0:1] / latents)).astype(BF16)


def finish(shares, own, dec_bias, norm_total, groups, r_dev, latents):
    rows = own.shape[0] - r_dev
    width = own.shape[1]
    return pl.pallas_call(
        functools.partial(finish_kernel, len(shares), groups, latents),
        out_shape=[jax.ShapeDtypeStruct((rows // groups, width), BF16)] * groups
        + [jax.ShapeDtypeStruct((r_dev, width), BF16), jax.ShapeDtypeStruct((8, 128), F32)],
        in_specs=[VMEM_SPEC] * (3 + len(shares)),
        out_specs=[VMEM_SPEC] * (groups + 2),
        name="finish",
    )(own, dec_bias, norm_total, *shares)


def all_sum(value, axis, size):
    mask = 1
    while mask < size:
        value = value + shift_to(value, axis, size, mask)
        mask *= 2
    return value


def body(residuals, topk_slots, dictionary, enc_bias, dec_bias, dead_ids, seed_tokens):
    tok_dev = residuals.shape[1]
    lat_count = lax.axis_size("lat")
    groups = lax.axis_size("layer")
    shard = lax.axis_index("lat")
    group = lax.axis_index("layer")
    lat_dev = dictionary.shape[1]
    slot_count = topk_slots.shape[2]
    per_shard = slot_count // lat_count
    r_dev = seed_tokens.shape[1] // lat_count
    outer, inner = split_lat(lat_count)

    packed = pack(group.reshape(1), residuals, topk_slots, per_shard, lat_dev)
    mine = jnp.concatenate(
        [packed[0]] + [shift_to(packed[k], "layer", groups, k) for k in range(1, groups)], axis=0
    )

    columns = [mine] + [shift_to(mine, "lat", lat_count, inner * z) for z in range(1, outer)]
    blocks = [
        block
        for column in columns
        for block in [column] + [shift_to(column, "lat", lat_count, x) for x in range(1, inner)]
    ]

    cols, norm_part = norms(dictionary[0], enc_bias, dec_bias, 512)
    norm_total = all_sum(norm_part, "lat", lat_count)

    unit = seed_tokens[0] // tok_dev
    tok_group = tok_dev * groups
    place = (
        jnp.bitwise_xor(unit % lat_count, shard) * tok_group
        + jnp.bitwise_xor(unit // lat_count, group) * tok_dev
        + seed_tokens[0] % tok_dev
    )
    order = jnp.bitwise_xor(jnp.arange(lat_count), shard)
    place = place.reshape(lat_count, r_dev)[order].reshape(1, -1)

    results = main(shard.reshape(1), place, dictionary[0], cols, blocks, per_shard, slot_count, 512)
    shares = results[:lat_count]
    normed, own, mass = results[lat_count:]

    sums = [None] * outer
    for z in reversed(range(outer)):
        total = shares[z * inner].astype(F32)
        for x in range(1, inner):
            total = total + shift_to(shares[z * inner + x], "lat", lat_count, x).astype(F32)
        sums[z] = total
    final = [sums[0]] + [shift_to(sums[z].astype(BF16), "lat", lat_count, inner * z) for z in range(1, outer)]

    *recon, new_rows, numerator = finish(final, own, dec_bias, norm_total, groups, r_dev, lat_dev * lat_count)
    numerator = all_sum(numerator, "lat", lat_count)[0, 0]
    returned = jnp.stack([recon[0]] + [shift_to(recon[k], "layer", groups, k) for k in range(1, groups)])
    reconstruction = returned[jnp.bitwise_xor(jnp.arange(groups), group)]

    feat32 = normed.astype(F32)
    centered = feat32 - jnp.mean(feat32, axis=0)
    unexplained = (numerator / jnp.sum(jnp.square(centered))).reshape(1)
    candidates = shard * lat_dev + jnp.arange(lat_dev, dtype=jnp.int32)
    is_dead = jnp.any(dead_ids[0][:, None] == candidates[None, :], axis=0)
    new_bias = jnp.where(is_dead, 0.0, enc_bias[0])[None]
    return (reconstruction, unexplained, mass, new_rows[None], new_bias)


def solution(mesh):
    in_specs = (
        P(None, ("layer", "lat"), None),
        P(None, ("layer", "lat"), None),
        P("layer", "lat", None),
        P("layer", "lat"),
        P("layer", None),
        P("layer", None),
        P("layer", None),
    )
    out_specs = (
        P(None, ("layer", "lat"), None),
        P("layer"),
        P("layer", "lat"),
        P("layer", "lat", None),
        P("layer", "lat"),
    )
    return jax.shard_map(body, mesh=mesh, in_specs=in_specs, out_specs=out_specs, check_vma=False)
```

```python
import functools
import jax
import jax.numpy as jnp
from jax import lax
from jax.experimental import pallas as pl
from jax.experimental.pallas import tpu as pltpu
from jax.sharding import PartitionSpec as P

F32 = jnp.float32
BF16 = jnp.bfloat16
LOW = 64
VMEM_SPEC = pl.BlockSpec(memory_space=pltpu.VMEM)
SMEM_SPEC = pl.BlockSpec(memory_space=pltpu.SMEM)
HBM_SPEC = pl.BlockSpec(memory_space=pltpu.HBM)


def split_lat(count):
    inner = 1
    while inner * inner * 4 <= count and count % (inner * 2) == 0:
        inner *= 2
    return count // inner, inner


def shift_to(value, axis, size, mask):
    return lax.ppermute(value, axis, [(i, i ^ mask) for i in range(size)])


def in_vmem(value):
    return pltpu.with_memory_space_constraint(value, pltpu.VMEM)


def in_hbm(value):
    return pltpu.with_memory_space_constraint(value, pltpu.HBM)


def pack_kernel(groups, per_shard, lat_dev, group_ref, res_hbm, slots_hbm, *refs):
    outs, (res_ref, slots_ref, sems) = refs[:groups], refs[groups:]
    copies = [
        pltpu.make_async_copy(slots_hbm, slots_ref, sems.at[0]),
        pltpu.make_async_copy(res_hbm, res_ref, sems.at[1]),
    ]
    for copy in copies:
        copy.start()
    for copy in copies:
        copy.wait()
    group = group_ref[1]
    width = res_ref.shape[2]
    slot_count = slots_ref.shape[2]
    shard = lax.broadcasted_iota(jnp.int32, slots_ref.shape[1:], 1) // per_shard
    for mask in range(groups):
        layer = jnp.bitwise_xor(group, mask)
        slots = slots_ref[layer]
        live = slots >= 0
        local = slots - shard * lat_dev
        high = jnp.where(live, local // LOW, -1)
        low = jnp.where(live, local % LOW, 0)
        outs[mask][:, :width] = res_ref[layer]
        outs[mask][:, width : width + 2 * slot_count] = jnp.concatenate([high, low], axis=1).astype(F32).astype(BF16)


def pack(group, residuals, slots, per_shard, lat_dev):
    groups, rows, width = residuals.shape
    return pl.pallas_call(
        functools.partial(pack_kernel, groups, per_shard, lat_dev),
        out_shape=[pltpu.VMEM((rows, width + 2 * slots.shape[2]), BF16)] * groups,
        in_specs=[SMEM_SPEC, HBM_SPEC, HBM_SPEC],
        out_specs=[VMEM_SPEC] * groups,
        scratch_shapes=[
            pltpu.VMEM(residuals.shape, residuals.dtype),
            pltpu.VMEM(slots.shape, slots.dtype),
            pltpu.SemaphoreType.DMA((2,)),
        ],
        compiler_params=pltpu.CompilerParams(vmem_limit_bytes=4 << 20),
        name="pack",
    )(group, in_hbm(residuals), in_hbm(slots))


def lane_to_line(column):
    eye = lax.broadcasted_iota(jnp.int32, (128, 128), 0) == lax.broadcasted_iota(jnp.int32, (128, 128), 1)
    return jnp.sum(jnp.where(eye, column, 0.0), axis=0, keepdims=True)


def load_kernel(first, rows, tile, after_ref, dict_ref, enc_hbm, dec_hbm, *refs):
    table_ref, lines_ref, total_ref, enc_ref, dec_ref, sems = refs[-6:]
    steps = rows // tile
    small = [
        pltpu.make_async_copy(enc_hbm.at[:, pl.ds(first, rows)], enc_ref, sems.at[steps]),
        pltpu.make_async_copy(dec_hbm, dec_ref, sems.at[steps + 1]),
    ]
    spans = [pl.ds(first + i * tile, tile) for i in range(steps)]
    copies = [pltpu.make_async_copy(dict_ref.at[span], table_ref.at[span], sems.at[i]) for i, span in enumerate(spans)]
    for copy in small + copies:
        copy.start()
    for copy in small:
        copy.wait()
    total = jnp.zeros((1, 1), F32) if first == 0 else refs[2][0:1, 0:1]
    for i in range(steps):
        copies[i].wait()
        for start in range(i * tile, (i + 1) * tile, 128):
            span = slice(first + start, first + start + 128)
            values = table_ref[span].astype(F32)
            norm = jnp.sqrt(lane_to_line(jnp.sum(values * values, axis=1, keepdims=True)) + 1e-06)
            shift = lane_to_line(jnp.sum(values * dec_ref[...], axis=1, keepdims=True))
            inverse = 1.0 / norm
            lines_ref[0:1, span] = inverse
            lines_ref[1:2, span] = enc_ref[:, start : start + 128] - shift * inverse
            total += jnp.sum(norm, keepdims=True)
    total_ref[...] = jnp.broadcast_to(total, total_ref.shape)


def load(before, after, dictionary, enc_bias, dec_bias, first, rows, tile):
    lat_dev, width = dictionary.shape
    return pl.pallas_call(
        functools.partial(load_kernel, first, rows, tile),
        out_shape=[
            pltpu.VMEM((lat_dev, width), BF16),
            pltpu.VMEM((2, lat_dev), F32),
            pltpu.VMEM((8, 128), F32),
        ],
        in_specs=[VMEM_SPEC, HBM_SPEC, HBM_SPEC, HBM_SPEC] + [VMEM_SPEC] * len(before),
        out_specs=[VMEM_SPEC] * 3,
        scratch_shapes=[
            pltpu.VMEM((1, rows), F32),
            pltpu.VMEM((1, width), F32),
            pltpu.SemaphoreType.DMA((rows // tile + 2,)),
        ],
        input_output_aliases={4 + i: i for i in range(len(before))},
        compiler_params=pltpu.CompilerParams(vmem_limit_bytes=24 << 20),
        name="load",
    )(
        in_vmem(after),
        in_hbm(dictionary),
        in_hbm(enc_bias),
        in_hbm(dec_bias),
        *[in_vmem(value) for value in before],
    )


def main_kernel(
    parts, blocks, outer, chunk, tok_dev, per_shard, slot_count, r_dev, tile, span, place_ref, seed_ref, *refs
):
    tables, refs = refs[:parts], refs[parts:]
    lines, refs = refs[:parts], refs[parts:]
    norm_parts, refs = refs[:parts], refs[parts:]
    ins, refs = refs[:blocks], refs[blocks:]
    shares, refs = refs[:blocks], refs[blocks:]
    inner = blocks // outer
    seed_shares, refs = refs[:inner], refs[inner:]
    normed, seed_features, norm_total, mass_ref, ids, weights, product, coefficients, chosen_rows = refs
    shard, group = place_ref[0], place_ref[1]
    part_rows, width = tables[0].shape
    rows = ins[0].shape[0]
    tokens = rows * blocks
    now = rows * chunk

    norm_total[...] = sum(part[...] for part in norm_parts)
    total = jnp.zeros((1, 1), F32)
    for block in ins:
        raw = block[:, :width].astype(F32)
        total += jnp.sum(raw * raw, keepdims=True)
    scale = lax.rsqrt(total / (tokens * width))
    for k, block in enumerate(ins):
        normed[k * rows : (k + 1) * rows, :] = (block[:, :width].astype(F32) * scale).astype(BF16)

    shape = (2 * slot_count, per_shard * 128)
    source = lax.broadcasted_iota(jnp.int32, shape, 0)
    wanted = lax.broadcasted_iota(jnp.int32, shape, 1) // 128 + shard * per_shard
    chooser = jnp.where(source == wanted, float(LOW), jnp.where(source == wanted + slot_count, 1.0, 0.0)).astype(BF16)
    lanes = [slice(c * 128, (c + 1) * 128) for c in range(per_shard)]
    lane = lax.broadcasted_iota(jnp.int32, (1, 128), 1)
    seeds = seed_ref[...]
    unit = seeds // tok_dev
    places = (
        jnp.bitwise_xor(unit % blocks, shard) * rows
        + jnp.bitwise_xor(unit // blocks, group) * tok_dev
        + seeds % tok_dev
    )
    rows_for = lambda k: pl.ds(pl.multiple_of(jnp.bitwise_xor(shard, k) * r_dev, r_dev), r_dev)
    place = lax.broadcasted_iota(jnp.int32, (tokens, r_dev * blocks), 0)
    chosen = jnp.where(place == places, 1.0, 0.0).astype(BF16)

    def pick(which, values):
        return lax.dot_general(which, values, (((0,), (0,)), ((), ())), preferred_element_type=F32).astype(BF16)

    chosen_rows[...] = pick(chosen, normed[...])
    seed_features[...] = chosen_rows[rows_for(0)]

    for lead in range(0, blocks, chunk):
        members = slice(lead * rows, lead * rows + now)
        coded = jnp.concatenate([block[:, width:] for block in ins[lead : lead + chunk]], axis=0)
        ids[...] = jnp.dot(coded, chooser, preferred_element_type=F32)
        for c in range(per_shard):
            weights[:, lanes[c]] = sum(jnp.where(ids[:, lanes[c]] == ids[:, other], 1.0, 0.0) for other in lanes)
        for part in range(parts):
            for first in range(0, part_rows, tile):
                product[...] = lax.dot_general(
                    normed[members],
                    tables[part][first : first + tile],
                    (((1,), (1,)), ((), ())),
                    preferred_element_type=F32,
                )
                for j in range(0, tile, 128):
                    local = slice(first + j, first + j + 128)
                    columns = slice(part * part_rows + first + j, part * part_rows + first + j + 128)
                    latent = (lane + columns.start).astype(F32)
                    inverse = lines[part][0:1, local]
                    offset = lines[part][1:2, local]
                    count = jnp.zeros((now, 128), F32)
                    for c in range(per_shard):
                        count = jnp.where(ids[:, lanes[c]] == latent, weights[:, lanes[c]], count)
                    activity = jnp.maximum(product[:, j : j + 128] * inverse + offset, 0.0)
                    mass = jnp.sum(activity * count, axis=0, keepdims=True)
                    mass_ref[:, columns] = mass if lead == 0 else mass_ref[:, columns] + mass
                    coefficients[:, columns] = (activity * inverse).astype(BF16) * count.astype(BF16)
        for start in range(0, width, span):
            columns = slice(start, start + span)
            share = sum(
                jnp.dot(
                    coefficients[:, part * part_rows : (part + 1) * part_rows],
                    tables[part][:, columns],
                    preferred_element_type=F32,
                )
                for part in range(parts)
            ).astype(BF16)
            picked = pick(chosen[members], share)
            chosen_rows[:, columns] = picked if lead == 0 else chosen_rows[:, columns] + picked
            for k in range(chunk):
                shares[lead + k][:, columns] = share[k * rows : (k + 1) * rows]
    for k in range(blocks):
        z, x = k // inner, k % inner
        seed_shares[x][z * r_dev : (z + 1) * r_dev] = chosen_rows[rows_for(k)]


def main(place, seeds, loaded, blocks, outer, tok_dev, per_shard, slot_count, tile, span):
    tables, lines, norm_parts = [[value] for value in loaded]
    part_rows, width = tables[0].shape
    parts = len(tables)
    lat_dev = part_rows * parts
    count = len(blocks)
    rows = blocks[0].shape[0]
    tokens = rows * count
    chunk = max(1, min(count, 512 // rows))
    now = chunk * rows
    r_dev = seeds.shape[1] // count
    arrays = [in_vmem(value) for value in (*tables, *lines, *norm_parts, *blocks)]
    results = pl.pallas_call(
        functools.partial(
            main_kernel, parts, count, outer, chunk, tok_dev, per_shard, slot_count, r_dev, tile, span
        ),
        out_shape=[pltpu.VMEM((rows, width), BF16)] * count
        + [pltpu.VMEM((outer * r_dev, width), BF16)] * (count // outer)
        + [
            pltpu.VMEM((tokens, width), BF16),
            pltpu.VMEM((r_dev, width), BF16),
            pltpu.VMEM((8, 128), F32),
            jax.ShapeDtypeStruct((1, lat_dev), F32),
        ],
        in_specs=[SMEM_SPEC, VMEM_SPEC] + [VMEM_SPEC] * len(arrays),
        out_specs=[VMEM_SPEC] * (count + count // outer + 4),
        scratch_shapes=[
            pltpu.VMEM((now, per_shard * 128), F32),
            pltpu.VMEM((now, per_shard * 128), F32),
            pltpu.VMEM((now, tile), F32),
            pltpu.VMEM((now, lat_dev), BF16),
            pltpu.VMEM((r_dev * count, width), BF16),
        ],
        compiler_params=pltpu.CompilerParams(vmem_limit_bytes=24 << 20),
        name="sparse_code",
    )(place, seeds, *arrays)
    return results[:count], results[count:-4], results[-4:]


def token_kernel(parts, groups, normed_ref, dec_ref, norm_ref, *refs):
    shares, refs = refs[:parts], refs[parts:]
    *recon, stats_ref = refs
    summed = shares[0][...].astype(F32)
    for share in shares[1:]:
        summed += share[...].astype(F32)
    estimate = summed + dec_ref[...]
    rows = estimate.shape[0]
    size = rows // groups
    for k in range(groups):
        recon[k][...] = estimate[k * size : (k + 1) * size].astype(BF16)
    errors = normed_ref[:rows].astype(F32) - estimate
    line = lax.broadcasted_iota(jnp.int32, stats_ref.shape, 0)
    stats_ref[...] = jnp.where(line == 0, jnp.sum(errors * errors, keepdims=True), norm_ref[...])


def finish_tokens(shares, normed, dec_bias, norm_part, groups):
    rows, width = shares[0].shape
    return pl.pallas_call(
        functools.partial(token_kernel, len(shares), groups),
        out_shape=[pltpu.VMEM((rows // groups, width), BF16)] * groups + [pltpu.VMEM((8, 128), F32)],
        in_specs=[VMEM_SPEC] * (3 + len(shares)),
        out_specs=[VMEM_SPEC] * (groups + 1),
        compiler_params=pltpu.CompilerParams(vmem_limit_bytes=8 << 20),
        name="finish_tokens",
    )(in_vmem(normed), dec_bias, in_vmem(norm_part), *[in_vmem(share) for share in shares])


def seed_sum_kernel(inner, *refs):
    shares, refs = refs[:inner], refs[inner:]
    stats, refs = refs[:inner], refs[inner:]
    mine_ref, stats_ref, *outs = refs
    r_dev, width = mine_ref.shape
    total = sum(stat[...] for stat in stats)
    stats_ref[...] = total
    line = jnp.zeros((1, 128), F32)
    lane = lax.broadcasted_iota(jnp.int32, (1, 128), 1)
    for which in range(2):
        rest = total[which : which + 1]
        for part in range(3):
            piece = rest.astype(BF16).astype(F32)
            line = jnp.where(lane == which * 3 + part, piece, line)
            rest = rest - piece
    line = jnp.broadcast_to(line, (r_dev, 128)).astype(BF16)
    for z, out in enumerate([mine_ref, *outs]):
        span = slice(z * r_dev, (z + 1) * r_dev)
        out[:, :width] = sum(share[span].astype(F32) for share in shares).astype(out.dtype)
        if z:
            out[:, width:] = line


def sum_seeds(shares, stats, outer):
    rows, width = shares[0].shape
    rows //= outer
    return pl.pallas_call(
        functools.partial(seed_sum_kernel, len(shares)),
        out_shape=[pltpu.VMEM((rows, width), F32), pltpu.VMEM((8, 128), F32)]
        + [pltpu.VMEM((rows, width + 128), BF16)] * (outer - 1),
        in_specs=[VMEM_SPEC] * (len(shares) + len(stats)),
        out_specs=[VMEM_SPEC] * (outer + 1),
        compiler_params=pltpu.CompilerParams(vmem_limit_bytes=8 << 20),
        name="sum_seeds",
    )(*[in_vmem(value) for value in (*shares, *stats)])


def seed_kernel(latents, features_ref, dec_ref, spread_ref, mine_ref, stats_ref, *refs):
    *shares, rows_ref, unexplained_ref = refs
    width = mine_ref.shape[1]
    summed = mine_ref[...]
    line = jnp.zeros((1, 128), F32)
    for share in shares:
        summed += share[:, :width].astype(F32)
        line += share[0:1, width:].astype(F32)
    lane = lax.broadcasted_iota(jnp.int32, (1, 128), 1)
    numerator = stats_ref[0:1, 0:1] + jnp.sum(jnp.where(lane < 3, line, 0.0), keepdims=True)
    norm_sum = stats_ref[1:2, 0:1] + jnp.sum(jnp.where((lane >= 3) & (lane < 6), line, 0.0), keepdims=True)
    seeds = features_ref[...].astype(F32) - (summed + dec_ref[...])
    norm = jnp.sqrt(jnp.sum(seeds * seeds, axis=1, keepdims=True) + 1e-06)
    rows_ref[...] = (seeds / norm * (norm_sum / latents)).astype(BF16)
    unexplained_ref[...] = numerator / spread_ref[...]


def finish_seeds(shares, features, dec_bias, spread, latents):
    return pl.pallas_call(
        functools.partial(seed_kernel, latents),
        out_shape=[jax.ShapeDtypeStruct(features.shape, BF16), jax.ShapeDtypeStruct((1, 1), F32)],
        in_specs=[VMEM_SPEC] * (3 + len(shares)),
        out_specs=[VMEM_SPEC] * 2,
        compiler_params=pltpu.CompilerParams(vmem_limit_bytes=8 << 20),
        name="finish_seeds",
    )(in_vmem(features), dec_bias, in_vmem(spread), *[in_vmem(value) for value in shares])


def side_kernel(chunk, place_ref, normed_ref, dead_ref, enc_ref, spread_ref, bias_ref):
    tokens, width = normed_ref.shape
    lat_dev = enc_ref.shape[1]
    total = jnp.zeros((1, 1), F32)
    for start in range(0, width, chunk):
        values = normed_ref[:, start : start + chunk].astype(F32)
        centered = values - jnp.sum(values, axis=0, keepdims=True) / tokens
        total += jnp.sum(centered * centered, keepdims=True)
    spread_ref[...] = total
    latent = lax.broadcasted_iota(jnp.int32, (1, lat_dev), 1) + place_ref[0] * lat_dev
    eye = lax.broadcasted_iota(jnp.int32, (128, 128), 0) == lax.broadcasted_iota(jnp.int32, (128, 128), 1)
    hits = jnp.zeros((1, lat_dev), jnp.int32)
    for start in range(0, dead_ref.shape[1], 128):
        dead = jnp.sum(jnp.where(eye, dead_ref[:, start : start + 128], 0), axis=1, keepdims=True)
        hits = jnp.maximum(hits, jnp.max(jnp.where(dead == latent, 1, 0), axis=0, keepdims=True))
    bias_ref[...] = jnp.where(hits > 0, 0.0, enc_ref[...])


def side(place, normed, dead_ids, enc_bias):
    return pl.pallas_call(
        functools.partial(side_kernel, 256),
        out_shape=[pltpu.VMEM((1, 1), F32), jax.ShapeDtypeStruct(enc_bias.shape, F32)],
        in_specs=[SMEM_SPEC] + [VMEM_SPEC] * 3,
        out_specs=[VMEM_SPEC] * 2,
        compiler_params=pltpu.CompilerParams(vmem_limit_bytes=8 << 20),
        name="side",
    )(place, in_vmem(normed), dead_ids, enc_bias)


def unpack_kernel(group_ref, *refs):
    *parts, out_ref = refs
    for mask, part in enumerate(parts):
        out_ref[jnp.bitwise_xor(group_ref[1], mask)] = part[...]


def unpack(group, parts):
    return pl.pallas_call(
        unpack_kernel,
        out_shape=jax.ShapeDtypeStruct((len(parts), *parts[0].shape), BF16),
        in_specs=[SMEM_SPEC] + [VMEM_SPEC] * len(parts),
        out_specs=VMEM_SPEC,
        compiler_params=pltpu.CompilerParams(vmem_limit_bytes=4 << 20),
        name="unpack",
    )(group, *[in_vmem(part) for part in parts])


LOADS = 4


def body(residuals, topk_slots, dictionary, enc_bias, dec_bias, dead_ids, seed_tokens):
    tok_dev = residuals.shape[1]
    lat_count = lax.axis_size("lat")
    groups = lax.axis_size("layer")
    shard = lax.axis_index("lat")
    group = lax.axis_index("layer")
    lat_dev = dictionary.shape[1]
    slot_count = topk_slots.shape[2]
    per_shard = slot_count // lat_count
    outer, inner = split_lat(lat_count)
    lat = lambda value, mask: shift_to(value, "lat", lat_count, mask)
    layer = lambda value, mask: shift_to(value, "layer", groups, mask)
    place = jnp.stack([shard, group])

    packed = pack(place, residuals, topk_slots, per_shard, lat_dev)
    mine = jnp.concatenate([packed[0]] + [layer(packed[k], k) for k in range(1, groups)], axis=0)
    columns = [mine] + [lat(mine, inner * z) for z in range(1, outer)]
    blocks = [block for column in columns for block in [column] + [lat(column, x) for x in range(1, inner)]]

    part_rows = lat_dev // LOADS
    loaded = ()
    for part, after in enumerate((packed[0], mine, columns[-1], columns[-1])):
        loaded = load(loaded, after, dictionary[0], enc_bias, dec_bias, part * part_rows, part_rows, part_rows // 4)
    shares, seed_shares, (normed, seed_features, norm_part, mass) = main(
        place, seed_tokens, loaded, blocks, outer, tok_dev, per_shard, slot_count, 1024, 1024
    )

    sums = [None] * outer
    for z in reversed(range(outer)):
        total = shares[z * inner].astype(F32)
        for x in range(1, inner):
            total = total + lat(shares[z * inner + x], x).astype(F32)
        sums[z] = total
    last = [sums[0]] + [lat(sums[z].astype(BF16), inner * z) for z in range(1, outer)]
    spread, new_bias = side(place, normed, dead_ids, enc_bias)
    *recon, stats = finish_tokens(last, normed, dec_bias, norm_part, groups)
    reconstruction = unpack(place, [recon[0]] + [layer(recon[k], k) for k in range(1, groups)])
    seed_sums = sum_seeds(
        [seed_shares[0]] + [lat(seed_shares[x], x) for x in range(1, inner)],
        [stats] + [lat(stats, x) for x in range(1, inner)],
        outer,
    )
    seed_last = list(seed_sums[:2]) + [lat(seed_sums[z + 1], inner * z) for z in range(1, outer)]
    new_rows, unexplained = finish_seeds(seed_last, seed_features, dec_bias, spread, lat_dev * lat_count)
    return (reconstruction, unexplained.reshape(1), mass, new_rows[None], new_bias)


def solution(mesh):
    in_specs = (
        P(None, ("layer", "lat"), None),
        P(None, ("layer", "lat"), None),
        P("layer", "lat", None),
        P("layer", "lat"),
        P("layer", None),
        P("layer", None),
        P("layer", None),
    )
    out_specs = (
        P(None, ("layer", "lat"), None),
        P("layer"),
        P("layer", "lat"),
        P("layer", "lat", None),
        P("layer", "lat"),
    )
    return jax.shard_map(body, mesh=mesh, in_specs=in_specs, out_specs=out_specs, check_vma=False)
```

```python
import functools
import jax
import jax.numpy as jnp
from jax import lax
from jax.experimental import pallas as pl
from jax.experimental.pallas import tpu as pltpu
from jax.sharding import PartitionSpec as P

F32 = jnp.float32
BF16 = jnp.bfloat16
LOW = 64
VMEM_SPEC = pl.BlockSpec(memory_space=pltpu.VMEM)
SMEM_SPEC = pl.BlockSpec(memory_space=pltpu.SMEM)
HBM_SPEC = pl.BlockSpec(memory_space=pltpu.HBM)


def split_lat(count):
    inner = 1
    while inner * inner * 4 <= count and count % (inner * 2) == 0:
        inner *= 2
    return count // inner, inner


def shift_to(value, axis, size, mask):
    return lax.ppermute(value, axis, [(i, i ^ mask) for i in range(size)])


def in_vmem(value):
    return pltpu.with_memory_space_constraint(value, pltpu.VMEM)


def in_hbm(value):
    return pltpu.with_memory_space_constraint(value, pltpu.HBM)


def pack_kernel(groups, per_shard, lat_dev, place_ref, res_hbm, slots_hbm, *refs):
    outs, (slots_ref, sems) = refs[:groups], refs[groups:]
    layers = [jnp.bitwise_xor(place_ref[1], mask) for mask in range(groups)]
    width = res_hbm.shape[2]
    slot_count = slots_ref.shape[2]
    slot_copy = pltpu.make_async_copy(slots_hbm, slots_ref, sems.at[groups])
    slot_copy.start()
    copies = [
        pltpu.make_async_copy(res_hbm.at[layer], out.at[:, pl.ds(0, width)], sems.at[mask])
        for mask, (layer, out) in enumerate(zip(layers, outs))
    ]
    for copy in copies:
        copy.start()
    slot_copy.wait()
    shard = lax.broadcasted_iota(jnp.int32, slots_ref.shape[1:], 1) // per_shard
    for layer, out in zip(layers, outs):
        slots = slots_ref[layer]
        live = slots >= 0
        local = slots - shard * lat_dev
        high = jnp.where(live, local // LOW, -1)
        low = jnp.where(live, local % LOW, 0)
        out[:, width : width + 2 * slot_count] = jnp.concatenate([high, low], axis=1).astype(F32).astype(BF16)
    for copy in copies:
        copy.wait()


def pack(place, residuals, slots, per_shard, lat_dev):
    groups, rows, width = residuals.shape
    return pl.pallas_call(
        functools.partial(pack_kernel, groups, per_shard, lat_dev),
        out_shape=[pltpu.VMEM((rows, width + 2 * slots.shape[2]), BF16)] * groups,
        in_specs=[SMEM_SPEC, HBM_SPEC, HBM_SPEC],
        out_specs=[VMEM_SPEC] * groups,
        scratch_shapes=[pltpu.VMEM(slots.shape, slots.dtype), pltpu.SemaphoreType.DMA((groups + 1,))],
        compiler_params=pltpu.CompilerParams(vmem_limit_bytes=4 << 20),
        name="pack",
    )(place, in_hbm(residuals), in_hbm(slots))


def lane_to_line(column):
    eye = lax.broadcasted_iota(jnp.int32, (128, 128), 0) == lax.broadcasted_iota(jnp.int32, (128, 128), 1)
    return jnp.sum(jnp.where(eye, column, 0.0), axis=0, keepdims=True)


def load_kernel(first, rows, tile, after_ref, dict_ref, enc_hbm, dec_hbm, *refs):
    table_ref, lines_ref, total_ref, enc_ref, dec_ref, sems = refs[-6:]
    steps = rows // tile
    small = [
        pltpu.make_async_copy(enc_hbm.at[:, pl.ds(first, rows)], enc_ref, sems.at[steps]),
        pltpu.make_async_copy(dec_hbm, dec_ref, sems.at[steps + 1]),
    ]
    spans = [pl.ds(first + i * tile, tile) for i in range(steps)]
    copies = [pltpu.make_async_copy(dict_ref.at[span], table_ref.at[span], sems.at[i]) for i, span in enumerate(spans)]
    for copy in small + copies:
        copy.start()
    for copy in small:
        copy.wait()
    total = jnp.zeros((1, 1), F32) if first == 0 else refs[2][0:1, 0:1]
    for i in range(steps):
        copies[i].wait()
        for start in range(i * tile, (i + 1) * tile, 128):
            span = slice(first + start, first + start + 128)
            values = table_ref[span].astype(F32)
            norm = jnp.sqrt(lane_to_line(jnp.sum(values * values, axis=1, keepdims=True)) + 1e-06)
            shift = lane_to_line(jnp.sum(values * dec_ref[...], axis=1, keepdims=True))
            inverse = 1.0 / norm
            lines_ref[0:1, span] = inverse
            lines_ref[1:2, span] = enc_ref[:, start : start + 128] - shift * inverse
            total += jnp.sum(norm, keepdims=True)
    total_ref[...] = jnp.broadcast_to(total, total_ref.shape)


def load(before, after, dictionary, enc_bias, dec_bias, first, rows, tile):
    lat_dev, width = dictionary.shape
    return pl.pallas_call(
        functools.partial(load_kernel, first, rows, tile),
        out_shape=[
            pltpu.VMEM((lat_dev, width), BF16),
            pltpu.VMEM((2, lat_dev), F32),
            pltpu.VMEM((8, 128), F32),
        ],
        in_specs=[VMEM_SPEC, HBM_SPEC, HBM_SPEC, HBM_SPEC] + [VMEM_SPEC] * len(before),
        out_specs=[VMEM_SPEC] * 3,
        scratch_shapes=[
            pltpu.VMEM((1, rows), F32),
            pltpu.VMEM((1, width), F32),
            pltpu.SemaphoreType.DMA((rows // tile + 2,)),
        ],
        input_output_aliases={4 + i: i for i in range(len(before))},
        compiler_params=pltpu.CompilerParams(vmem_limit_bytes=24 << 20),
        name="load",
    )(
        in_vmem(after),
        in_hbm(dictionary),
        in_hbm(enc_bias),
        in_hbm(dec_bias),
        *[in_vmem(value) for value in before],
    )


def main_kernel(
    parts, blocks, outer, chunk, tok_dev, per_shard, slot_count, r_dev, tile, span, place_ref, seed_ref, *refs
):
    tables, refs = refs[:parts], refs[parts:]
    lines, refs = refs[:parts], refs[parts:]
    norm_parts, refs = refs[:parts], refs[parts:]
    ins, refs = refs[:blocks], refs[blocks:]
    shares, refs = refs[:blocks], refs[blocks:]
    inner = blocks // outer
    seed_shares, refs = refs[:inner], refs[inner:]
    normed, seed_features, norm_total, mass_ref, ids, weights, product, coefficients, chosen_rows = refs
    shard, group = place_ref[0], place_ref[1]
    part_rows, width = tables[0].shape
    rows = ins[0].shape[0]
    tokens = rows * blocks
    now = rows * chunk

    norm_total[...] = sum(part[...] for part in norm_parts)
    total = jnp.zeros((1, 1), F32)
    for block in ins:
        raw = block[:, :width].astype(F32)
        total += jnp.sum(raw * raw, keepdims=True)
    scale = lax.rsqrt(total / (tokens * width))
    for k, block in enumerate(ins):
        normed[k * rows : (k + 1) * rows, :] = (block[:, :width].astype(F32) * scale).astype(BF16)

    shape = (2 * slot_count, per_shard * 128)
    source = lax.broadcasted_iota(jnp.int32, shape, 0)
    wanted = lax.broadcasted_iota(jnp.int32, shape, 1) // 128 + shard * per_shard
    chooser = jnp.where(source == wanted, float(LOW), jnp.where(source == wanted + slot_count, 1.0, 0.0)).astype(BF16)
    lanes = [slice(c * 128, (c + 1) * 128) for c in range(per_shard)]
    lane = lax.broadcasted_iota(jnp.int32, (1, 128), 1)
    seeds = seed_ref[...]
    unit = seeds // tok_dev
    places = (
        jnp.bitwise_xor(unit % blocks, shard) * rows
        + jnp.bitwise_xor(unit // blocks, group) * tok_dev
        + seeds % tok_dev
    )
    rows_for = lambda k: pl.ds(pl.multiple_of(jnp.bitwise_xor(shard, k) * r_dev, r_dev), r_dev)
    place = lax.broadcasted_iota(jnp.int32, (tokens, r_dev * blocks), 0)
    chosen = jnp.where(place == places, 1.0, 0.0).astype(BF16)

    def pick(which, values):
        return lax.dot_general(which, values, (((0,), (0,)), ((), ())), preferred_element_type=F32).astype(BF16)

    chosen_rows[...] = pick(chosen, normed[...])
    seed_features[...] = chosen_rows[rows_for(0)]

    for lead in range(0, blocks, chunk):
        members = slice(lead * rows, lead * rows + now)
        coded = jnp.concatenate([block[:, width:] for block in ins[lead : lead + chunk]], axis=0)
        ids[...] = jnp.dot(coded, chooser, preferred_element_type=F32)
        for c in range(per_shard):
            weights[:, lanes[c]] = sum(jnp.where(ids[:, lanes[c]] == ids[:, other], 1.0, 0.0) for other in lanes)
        for part in range(parts):
            for first in range(0, part_rows, tile):
                product[...] = lax.dot_general(
                    normed[members],
                    tables[part][first : first + tile],
                    (((1,), (1,)), ((), ())),
                    preferred_element_type=F32,
                )
                for j in range(0, tile, 128):
                    local = slice(first + j, first + j + 128)
                    columns = slice(part * part_rows + first + j, part * part_rows + first + j + 128)
                    latent = (lane + columns.start).astype(F32)
                    inverse = lines[part][0:1, local]
                    offset = lines[part][1:2, local]
                    count = jnp.zeros((now, 128), F32)
                    for c in range(per_shard):
                        count = jnp.where(ids[:, lanes[c]] == latent, weights[:, lanes[c]], count)
                    activity = jnp.maximum(product[:, j : j + 128] * inverse + offset, 0.0)
                    mass = jnp.sum(activity * count, axis=0, keepdims=True)
                    mass_ref[:, columns] = mass if lead == 0 else mass_ref[:, columns] + mass
                    coefficients[:, columns] = (activity * inverse).astype(BF16) * count.astype(BF16)
        for start in range(0, width, span):
            columns = slice(start, start + span)
            share = sum(
                jnp.dot(
                    coefficients[:, part * part_rows : (part + 1) * part_rows],
                    tables[part][:, columns],
                    preferred_element_type=F32,
                )
                for part in range(parts)
            ).astype(BF16)
            picked = pick(chosen[members], share)
            chosen_rows[:, columns] = picked if lead == 0 else chosen_rows[:, columns] + picked
            for k in range(chunk):
                shares[lead + k][:, columns] = share[k * rows : (k + 1) * rows]
    for k in range(blocks):
        z, x = k // inner, k % inner
        seed_shares[x][z * r_dev : (z + 1) * r_dev] = chosen_rows[rows_for(k)]


def main(place, seeds, loaded, blocks, outer, tok_dev, per_shard, slot_count, tile, span):
    tables, lines, norm_parts = [[value] for value in loaded]
    part_rows, width = tables[0].shape
    parts = len(tables)
    lat_dev = part_rows * parts
    count = len(blocks)
    rows = blocks[0].shape[0]
    tokens = rows * count
    chunk = max(1, min(count, 512 // rows))
    now = chunk * rows
    r_dev = seeds.shape[1] // count
    arrays = [in_vmem(value) for value in (*tables, *lines, *norm_parts, *blocks)]
    results = pl.pallas_call(
        functools.partial(
            main_kernel, parts, count, outer, chunk, tok_dev, per_shard, slot_count, r_dev, tile, span
        ),
        out_shape=[pltpu.VMEM((rows, width), BF16)] * count
        + [pltpu.VMEM((outer * r_dev, width), BF16)] * (count // outer)
        + [
            pltpu.VMEM((tokens, width), BF16),
            pltpu.VMEM((r_dev, width), BF16),
            pltpu.VMEM((8, 128), F32),
            jax.ShapeDtypeStruct((1, lat_dev), F32),
        ],
        in_specs=[SMEM_SPEC, VMEM_SPEC] + [VMEM_SPEC] * len(arrays),
        out_specs=[VMEM_SPEC] * (count + count // outer + 4),
        scratch_shapes=[
            pltpu.VMEM((now, per_shard * 128), F32),
            pltpu.VMEM((now, per_shard * 128), F32),
            pltpu.VMEM((now, tile), F32),
            pltpu.VMEM((now, lat_dev), BF16),
            pltpu.VMEM((r_dev * count, width), BF16),
        ],
        compiler_params=pltpu.CompilerParams(vmem_limit_bytes=24 << 20),
        name="sparse_code",
    )(place, seeds, *arrays)
    return results[:count], results[count:-4], results[-4:]


def token_kernel(parts, groups, normed_ref, dec_ref, norm_ref, *refs):
    shares, refs = refs[:parts], refs[parts:]
    *recon, stats_ref = refs
    summed = shares[0][...].astype(F32)
    for share in shares[1:]:
        summed += share[...].astype(F32)
    estimate = summed + dec_ref[...]
    rows = estimate.shape[0]
    size = rows // groups
    for k in range(groups):
        recon[k][...] = estimate[k * size : (k + 1) * size].astype(BF16)
    errors = normed_ref[:rows].astype(F32) - estimate
    line = lax.broadcasted_iota(jnp.int32, stats_ref.shape, 0)
    stats_ref[...] = jnp.where(line == 0, jnp.sum(errors * errors, keepdims=True), norm_ref[...])


def finish_tokens(shares, normed, dec_bias, norm_part, groups):
    rows, width = shares[0].shape
    return pl.pallas_call(
        functools.partial(token_kernel, len(shares), groups),
        out_shape=[pltpu.VMEM((rows // groups, width), BF16)] * groups + [pltpu.VMEM((8, 128), F32)],
        in_specs=[VMEM_SPEC] * (3 + len(shares)),
        out_specs=[VMEM_SPEC] * (groups + 1),
        compiler_params=pltpu.CompilerParams(vmem_limit_bytes=8 << 20),
        name="finish_tokens",
    )(in_vmem(normed), dec_bias, in_vmem(norm_part), *[in_vmem(share) for share in shares])


def seed_sum_kernel(inner, *refs):
    shares, refs = refs[:inner], refs[inner:]
    stats, refs = refs[:inner], refs[inner:]
    mine_ref, stats_ref, *outs = refs
    r_dev, width = mine_ref.shape
    total = sum(stat[...] for stat in stats)
    stats_ref[...] = total
    line = jnp.zeros((1, 128), F32)
    lane = lax.broadcasted_iota(jnp.int32, (1, 128), 1)
    for which in range(2):
        rest = total[which : which + 1]
        for part in range(3):
            piece = rest.astype(BF16).astype(F32)
            line = jnp.where(lane == which * 3 + part, piece, line)
            rest = rest - piece
    line = jnp.broadcast_to(line, (r_dev, 128)).astype(BF16)
    for z, out in enumerate([mine_ref, *outs]):
        span = slice(z * r_dev, (z + 1) * r_dev)
        out[:, :width] = sum(share[span].astype(F32) for share in shares).astype(out.dtype)
        if z:
            out[:, width:] = line


def sum_seeds(shares, stats, outer):
    rows, width = shares[0].shape
    rows //= outer
    return pl.pallas_call(
        functools.partial(seed_sum_kernel, len(shares)),
        out_shape=[pltpu.VMEM((rows, width), F32), pltpu.VMEM((8, 128), F32)]
        + [pltpu.VMEM((rows, width + 128), BF16)] * (outer - 1),
        in_specs=[VMEM_SPEC] * (len(shares) + len(stats)),
        out_specs=[VMEM_SPEC] * (outer + 1),
        compiler_params=pltpu.CompilerParams(vmem_limit_bytes=8 << 20),
        name="sum_seeds",
    )(*[in_vmem(value) for value in (*shares, *stats)])


def seed_kernel(latents, features_ref, dec_ref, spread_ref, mine_ref, stats_ref, *refs):
    *shares, rows_ref, unexplained_ref = refs
    width = mine_ref.shape[1]
    summed = mine_ref[...]
    line = jnp.zeros((1, 128), F32)
    for share in shares:
        summed += share[:, :width].astype(F32)
        line += share[0:1, width:].astype(F32)
    lane = lax.broadcasted_iota(jnp.int32, (1, 128), 1)
    numerator = stats_ref[0:1, 0:1] + jnp.sum(jnp.where(lane < 3, line, 0.0), keepdims=True)
    norm_sum = stats_ref[1:2, 0:1] + jnp.sum(jnp.where((lane >= 3) & (lane < 6), line, 0.0), keepdims=True)
    seeds = features_ref[...].astype(F32) - (summed + dec_ref[...])
    norm = jnp.sqrt(jnp.sum(seeds * seeds, axis=1, keepdims=True) + 1e-06)
    rows_ref[...] = (seeds / norm * (norm_sum / latents)).astype(BF16)
    unexplained_ref[...] = numerator / spread_ref[...]


def finish_seeds(shares, features, dec_bias, spread, latents):
    return pl.pallas_call(
        functools.partial(seed_kernel, latents),
        out_shape=[jax.ShapeDtypeStruct(features.shape, BF16), jax.ShapeDtypeStruct((1, 1), F32)],
        in_specs=[VMEM_SPEC] * (3 + len(shares)),
        out_specs=[VMEM_SPEC] * 2,
        compiler_params=pltpu.CompilerParams(vmem_limit_bytes=8 << 20),
        name="finish_seeds",
    )(in_vmem(features), dec_bias, in_vmem(spread), *[in_vmem(value) for value in shares])


def side_kernel(chunk, place_ref, normed_ref, dead_ref, enc_ref, spread_ref, bias_ref):
    tokens, width = normed_ref.shape
    lat_dev = enc_ref.shape[1]
    total = jnp.zeros((1, 1), F32)
    for start in range(0, width, chunk):
        values = normed_ref[:, start : start + chunk].astype(F32)
        centered = values - jnp.sum(values, axis=0, keepdims=True) / tokens
        total += jnp.sum(centered * centered, keepdims=True)
    spread_ref[...] = total
    latent = lax.broadcasted_iota(jnp.int32, (1, lat_dev), 1) + place_ref[0] * lat_dev
    eye = lax.broadcasted_iota(jnp.int32, (128, 128), 0) == lax.broadcasted_iota(jnp.int32, (128, 128), 1)
    hits = jnp.zeros((1, lat_dev), jnp.int32)
    for start in range(0, dead_ref.shape[1], 128):
        dead = jnp.sum(jnp.where(eye, dead_ref[:, start : start + 128], 0), axis=1, keepdims=True)
        hits = jnp.maximum(hits, jnp.max(jnp.where(dead == latent, 1, 0), axis=0, keepdims=True))
    bias_ref[...] = jnp.where(hits > 0, 0.0, enc_ref[...])


def side(place, normed, dead_ids, enc_bias):
    return pl.pallas_call(
        functools.partial(side_kernel, 256),
        out_shape=[pltpu.VMEM((1, 1), F32), jax.ShapeDtypeStruct(enc_bias.shape, F32)],
        in_specs=[SMEM_SPEC] + [VMEM_SPEC] * 3,
        out_specs=[VMEM_SPEC] * 2,
        compiler_params=pltpu.CompilerParams(vmem_limit_bytes=8 << 20),
        name="side",
    )(place, in_vmem(normed), dead_ids, enc_bias)


def unpack_kernel(group_ref, *refs):
    *parts, out_ref = refs
    for mask, part in enumerate(parts):
        out_ref[jnp.bitwise_xor(group_ref[1], mask)] = part[...]


def unpack(group, parts):
    return pl.pallas_call(
        unpack_kernel,
        out_shape=jax.ShapeDtypeStruct((len(parts), *parts[0].shape), BF16),
        in_specs=[SMEM_SPEC] + [VMEM_SPEC] * len(parts),
        out_specs=VMEM_SPEC,
        compiler_params=pltpu.CompilerParams(vmem_limit_bytes=4 << 20),
        name="unpack",
    )(group, *[in_vmem(part) for part in parts])


def body(residuals, topk_slots, dictionary, enc_bias, dec_bias, dead_ids, seed_tokens):
    tok_dev = residuals.shape[1]
    lat_count = lax.axis_size("lat")
    groups = lax.axis_size("layer")
    shard = lax.axis_index("lat")
    group = lax.axis_index("layer")
    lat_dev = dictionary.shape[1]
    slot_count = topk_slots.shape[2]
    per_shard = slot_count // lat_count
    outer, inner = split_lat(lat_count)
    lat = lambda value, mask: shift_to(value, "lat", lat_count, mask)
    layer = lambda value, mask: shift_to(value, "layer", groups, mask)
    place = jnp.stack([shard, group])

    packed = pack(place, residuals, topk_slots, per_shard, lat_dev)
    mine = jnp.concatenate([packed[0]] + [layer(packed[k], k) for k in range(1, groups)], axis=0)
    columns = [mine] + [lat(mine, inner * z) for z in range(1, outer)]
    blocks = [block for column in columns for block in [column] + [lat(column, x) for x in range(1, inner)]]

    loaded, first = (), 0
    for after, rows in ((mine, lat_dev // 2), (columns[-1], lat_dev // 2)):
        loaded = load(loaded, after, dictionary[0], enc_bias, dec_bias, first, rows, lat_dev // 16)
        first += rows
    shares, seed_shares, (normed, seed_features, norm_part, mass) = main(
        place, seed_tokens, loaded, blocks, outer, tok_dev, per_shard, slot_count, 2048, 1024
    )

    sums = [None] * outer
    for z in reversed(range(outer)):
        total = shares[z * inner].astype(F32)
        for x in range(1, inner):
            total = total + lat(shares[z * inner + x], x).astype(F32)
        sums[z] = total
    last = [sums[0]] + [lat(sums[z].astype(BF16), inner * z) for z in range(1, outer)]
    spread, new_bias = side(place, normed, dead_ids, enc_bias)
    *recon, stats = finish_tokens(last, normed, dec_bias, norm_part, groups)
    reconstruction = unpack(place, [recon[0]] + [layer(recon[k], k) for k in range(1, groups)])
    seed_sums = sum_seeds(
        [seed_shares[0]] + [lat(seed_shares[x], x) for x in range(1, inner)],
        [stats] + [lat(stats, x) for x in range(1, inner)],
        outer,
    )
    seed_last = list(seed_sums[:2]) + [lat(seed_sums[z + 1], inner * z) for z in range(1, outer)]
    new_rows, unexplained = finish_seeds(seed_last, seed_features, dec_bias, spread, lat_dev * lat_count)
    return (reconstruction, unexplained.reshape(1), mass, new_rows[None], new_bias)


def solution(mesh):
    in_specs = (
        P(None, ("layer", "lat"), None),
        P(None, ("layer", "lat"), None),
        P("layer", "lat", None),
        P("layer", "lat"),
        P("layer", None),
        P("layer", None),
        P("layer", None),
    )
    out_specs = (
        P(None, ("layer", "lat"), None),
        P("layer"),
        P("layer", "lat"),
        P("layer", "lat", None),
        P("layer", "lat"),
    )
    return jax.shard_map(body, mesh=mesh, in_specs=in_specs, out_specs=out_specs, check_vma=False)
```
